32 devices in a mesh: tile: 16 (over z, y, x), band: 2 (over core).
Axes of the slice: x: 2, y: 2, z: 4, core: 2. Of those that a mesh axis runs over, the one named last changes fastest.
Arguments:
- voxel_feat: bfloat16 [4096, 64, 256], P(('tile', 'band')), may hold values from -6 to 6
- window_count: int32 [4096], P(('tile', 'band')), may hold values from 1 to 64
- voxel_cell: int32 [4096, 64], P(('tile', 'band')), may hold values from 0 to 2047
- w_qkv_voxel: bfloat16 [256, 768], replicated, may hold values from -1 to 1
- w_out_voxel: bfloat16 [256, 256], replicated, may hold values from -0.375 to 0.375
- w_up_voxel: bfloat16 [256, 512], replicated, may hold values from -0.375 to 0.375
- w_down_voxel: bfloat16 [512, 256], replicated, may hold values from -0.25 to 0.25
- conv_taps: float32 [9, 256], replicated, may hold values from -2 to 2
- w_qkv_bev: bfloat16 [256, 768], replicated, may hold values from -1 to 1
- w_out_bev: bfloat16 [256, 256], replicated, may hold values from -0.375 to 0.375
- w_up_bev: bfloat16 [256, 512], replicated, may hold values from -0.375 to 0.375
- w_down_bev: bfloat16 [512, 256], replicated, may hold values from -0.25 to 0.25
Outputs:
- bev_out: bfloat16 [256, 128, 256], P(('tile', 'band'))
The draws below stay inside these ranges and needn't reach their ends.
Inputs may be any that keep to these rules, and one draw needn't show every extreme that they name: The live slots of a window are its first window_count slots. `voxel_cell`: read only for live slots.
All inputs are finite; a program needn't handle non-finite values.
Results may differ from the reference program's by a relative error of at most 0.035.
Values may be sent and summed in bfloat16 or wider, within the bound.
A program may use at most 192 MiB of HBM per device.

```python
import jax
import jax.numpy as jnp
from jax import lax

D = 256
HEADS = 8
FF = 512
SLOT = 64
WSIDE = 8
WIN = 128
CB = 8
WINDOWS = 4096
TILE_CELLS = 2048
N_TILE = 16
N_BAND = 2


def projection_matrix(key):
    entries = jax.random.normal(key, (D, 3 * D), jnp.float32) * D ** (-0.5)
    entries = jnp.clip(entries, -6.0 * D ** (-0.5), 6.0 * D ** (-0.5))
    return entries.astype(jnp.bfloat16)


def draw_w_qkv_voxel(key, part):
    return projection_matrix(jax.random.fold_in(key, 101))


def draw_w_qkv_bev(key, part):
    return projection_matrix(jax.random.fold_in(key, 202))


def set_ends(array, key, low, largest):
    place = [jax.random.randint(jax.random.fold_in(key, axis), (), 0, length) for axis, length in enumerate(array.shape)]
    widest = array.shape.index(max(array.shape))
    neighbour = place[:widest] + [(place[widest] + 1) % array.shape[widest]] + place[widest + 1:]
    return array.at[tuple(place)].set(low).at[tuple(neighbour)].set(largest)


def block_levels(stream_key, shape, shards, smallest, high):
    def one(dim, parts):
        steps = jax.random.uniform(jax.random.fold_in(jax.random.fold_in(stream_key, 6), dim), (parts,), jnp.float32, smallest / len(shards), high / len(shards))
        return jnp.repeat(jnp.exp(steps), shape[dim] // parts).reshape((-1,) + (1,) * (len(shape) - dim - 1))

    factor_of = one(*shards[0])
    for cut in shards[1:]:
        factor_of = factor_of * one(*cut)
    return factor_of


def noise(own_key, dims, deviation, reach, shards=(), kind=jnp.bfloat16):
    values = jax.random.normal(own_key, dims, jnp.float32) * deviation
    if len(shards) > 0:
        values = block_levels(own_key, dims, shards, -0.22, 0.18) * values
    return jnp.clip(values, min=-reach, max=reach).astype(kind)


def setup_inputs(seed: int = 0) -> dict:
    key_list = jax.random.split(jax.random.key(seed), 13)
    return {
        "voxel_feat": noise(key_list[0], (WINDOWS, SLOT, D), 1.0, 6.0, ((0, 32),)),
        "window_count": set_ends(jax.random.randint(key_list[1], (WINDOWS,), 1, SLOT + 1), jax.random.fold_in(key_list[1], 1), 1, SLOT).astype(jnp.int32),
        "voxel_cell": set_ends(jax.random.randint(key_list[2], (WINDOWS, SLOT), 0, TILE_CELLS), jax.random.fold_in(key_list[2], 1), 0, TILE_CELLS - 1).astype(jnp.int32),
        "w_qkv_voxel": draw_w_qkv_voxel(jax.random.fold_in(key_list[12], 71), 0),
        "w_out_voxel": noise(key_list[4], (D, D), D ** -0.5, 0.375),
        "w_up_voxel": noise(key_list[5], (D, FF), D ** -0.5, 0.375),
        "w_down_voxel": noise(key_list[6], (FF, D), FF ** -0.5, 0.25),
        "conv_taps": noise(key_list[7], (9, D), 9 ** -0.5, 2.0, (), jnp.float32),
        "w_qkv_bev": draw_w_qkv_bev(jax.random.fold_in(key_list[12], 71), 0),
        "w_out_bev": noise(key_list[9], (D, D), D ** -0.5, 0.375),
        "w_up_bev": noise(key_list[10], (D, FF), D ** -0.5, 0.375),
        "w_down_bev": noise(key_list[11], (FF, D), FF ** -0.5, 0.25),
    }


def layer_norm(values):
    center = values - lax.optimization_barrier(jnp.mean(values, axis=-1, keepdims=True))
    spread = lax.optimization_barrier(jnp.mean(center * center, axis=-1, keepdims=True))
    return center * lax.rsqrt(spread + 1e-05)

def attend_block(windows, keep, w_qkv, w_out, w_up, w_down):
    groups, slots, width = windows.shape
    head_dim = width // HEADS
    packed = jnp.einsum('gsd,de->gse', windows.astype(jnp.float32), w_qkv.astype(jnp.float32)).astype(jnp.bfloat16)
    queries = packed[:, :, :width].reshape(groups, slots, HEADS, head_dim)
    keys_part = packed[:, :, width:2 * width].reshape(groups, slots, HEADS, head_dim)
    vals_part = packed[:, :, 2 * width:].reshape(groups, slots, HEADS, head_dim)
    scores = jnp.einsum('gqhe,gkhe->ghqk', queries.astype(jnp.float32), keys_part.astype(jnp.float32)) * head_dim ** (-0.5)
    if keep is not None:
        scores = jnp.where(keep[:, None, None, :], scores, -1e+30)
    top = lax.optimization_barrier(jnp.max(scores, axis=-1, keepdims=True))
    raised = jnp.exp(scores - top)
    weights = (raised / lax.optimization_barrier(jnp.sum(raised, axis=-1, keepdims=True))).astype(jnp.bfloat16)
    mixed = jnp.einsum('ghqk,gkhe->gqhe', weights.astype(jnp.float32), vals_part.astype(jnp.float32)).astype(jnp.bfloat16)
    mixed = mixed.reshape(groups, slots, width)
    projected = jnp.einsum('gsd,de->gse', mixed.astype(jnp.float32), w_out.astype(jnp.float32))
    hidden = layer_norm(windows.astype(jnp.float32) + projected).astype(jnp.bfloat16)
    lifted = jax.nn.relu(jnp.einsum('gsd,de->gse', hidden.astype(jnp.float32), w_up.astype(jnp.float32))).astype(jnp.bfloat16)
    lowered = jnp.einsum('gsf,fd->gsd', lifted.astype(jnp.float32), w_down.astype(jnp.float32))
    return layer_norm(hidden.astype(jnp.float32) + lowered).astype(jnp.bfloat16)

def reference(voxel_feat, window_count, voxel_cell, w_qkv_voxel, w_out_voxel, w_up_voxel, w_down_voxel, conv_taps, w_qkv_bev, w_out_bev, w_up_bev, w_down_bev):
    n_groups = N_TILE * N_BAND
    rows = WSIDE * n_groups
    cols = CB * N_TILE
    slot_ids = jnp.arange(SLOT, dtype=jnp.int32)
    keep_all = slot_ids[None, :] < window_count[:, None]
    grouped = voxel_feat.reshape(n_groups, WIN, SLOT, D)
    keep_grouped = keep_all.reshape(n_groups, WIN, SLOT)

    def first_section(pair):
        return attend_block(pair[0], pair[1], w_qkv_voxel, w_out_voxel, w_up_voxel, w_down_voxel)
    encoded = lax.map(first_section, (grouped, keep_grouped)).reshape(n_groups * WIN, SLOT, D)
    window_ids = jnp.arange(n_groups * WIN, dtype=jnp.int32)
    group_of = window_ids // WIN
    tile_of = group_of // N_BAND
    band_of = group_of % N_BAND
    cell_row = voxel_cell // CB
    cell_col = voxel_cell % CB + tile_of[:, None] * CB
    target = band_of[:, None] * (rows * cols) + cell_row * cols + cell_col
    target = jnp.where(keep_all, target, N_BAND * rows * cols).astype(jnp.int32)
    pooled = jax.ops.segment_sum(encoded.reshape(-1, D).astype(jnp.float32), target.reshape(-1), num_segments=N_BAND * rows * cols + 1)
    per_band = pooled[:-1].astype(jnp.bfloat16).reshape(N_BAND, rows, cols, D)
    total = per_band[0].astype(jnp.float32) + per_band[1].astype(jnp.float32)
    bev = layer_norm(total).astype(jnp.bfloat16)
    padded = jnp.pad(bev, ((1, 1), (1, 1), (0, 0)))
    position = jnp.zeros((rows, cols, D), jnp.float32)
    for row_tap in range(3):
        for col_tap in range(3):
            position = position + padded[row_tap:row_tap + rows, col_tap:col_tap + cols].astype(jnp.float32) * conv_taps[3 * row_tap + col_tap].astype(jnp.float32)
    shaped = (bev.astype(jnp.float32) + position).astype(jnp.bfloat16)
    across = cols // WSIDE
    windows = shaped.reshape(n_groups, WSIDE, across, WSIDE, D).transpose(0, 2, 1, 3, 4).reshape(n_groups, across, WSIDE * WSIDE, D)

    def second_section(strip):
        return attend_block(strip, None, w_qkv_bev, w_out_bev, w_up_bev, w_down_bev)
    result = lax.map(second_section, windows)
    result = result.reshape(n_groups, across, WSIDE, WSIDE, D).transpose(0, 2, 1, 3, 4).reshape(rows, cols, D)
    return result
```

```python
import functools
import math

import jax
import jax.numpy as jnp
from jax import lax
from jax.experimental import pallas as pl
from jax.experimental.pallas import tpu as pltpu
from jax.sharding import PartitionSpec as P

HEADS = 8
WSIDE = 8
CB = 8
LANES = 128


def swapped(x, axis, bit):
    return lax.ppermute(x, axis, [(i, i ^ 1 << bit) for i in range(lax.axis_size(axis))])


def with_halo(block, sides, width):
    for axis, dim in sides:
        count = lax.axis_size(axis)
        forward = [(i, i + 1) for i in range(count - 1)]
        backward = [(target, source) for source, target in forward]
        low = lax.ppermute(
            lax.slice_in_dim(block, block.shape[dim] - width, None, axis=dim), axis, forward
        )
        high = lax.ppermute(lax.slice_in_dim(block, 0, width, axis=dim), axis, backward)
        block = jnp.concatenate([low, block, high], axis=dim)
    return block


def layer_norm(values, axis=-1):
    center = values - jnp.mean(values, axis=axis, keepdims=True)
    spread = jnp.mean(center * center, axis=axis, keepdims=True)
    return center * lax.rsqrt(spread + 1e-05)


def dot(a, b, contract=(1, 0)):
    return lax.dot_general(
        a, b, (((contract[0],), (contract[1],)), ((), ())), preferred_element_type=jnp.float32
    )


def attend_columns(x, counts, w_qv, w_k, w_out, w_up, w_down):
    tokens, width = x.shape
    head_dim = width // HEADS
    half_heads = LANES // head_dim
    slots = LANES // 2
    factor = head_dim ** (-0.5) * math.log2(math.e)
    turned = dot(w_qv, x, (1, 1))
    queries = turned[:width].astype(jnp.bfloat16)
    vals = turned[width:]
    keys = dot(x, w_k).astype(jnp.bfloat16)
    lane = lax.broadcasted_iota(jnp.int32, (LANES, LANES), 1)
    row = lax.broadcasted_iota(jnp.int32, (LANES, LANES), 0)
    first = lane < slots
    first_b = first.astype(jnp.bfloat16)
    second_b = 1 - first_b
    key_head = lane[:slots] // head_dim
    key_masks = [(key_head == h).astype(jnp.bfloat16) for h in range(half_heads)]
    val_masks = [
        (row // head_dim == 2 * j + lane // slots).astype(jnp.bfloat16)
        for j in range(half_heads // 2)
    ]
    mixed = []
    for pair in range(tokens // LANES):
        at = pair * LANES
        if counts is not None:
            limit = jnp.where(first[:slots], counts(2 * pair), counts(2 * pair + 1))
            bias = jnp.where(row[:slots] < limit, 0.0, -1e30)
        halves = []
        for half in range(width // LANES):
            f = half * LANES
            q = queries[f : f + LANES, at : at + LANES]
            q_blocks = jnp.concatenate([q * first_b, q * second_b], axis=0)
            k_blocks = jnp.concatenate(
                [
                    jnp.concatenate(
                        [
                            keys[at + w * slots : at + (w + 1) * slots, f : f + LANES] * m
                            for m in key_masks
                        ],
                        axis=0,
                    )
                    for w in range(2)
                ],
                axis=1,
            )
            scores = dot(k_blocks, q_blocks).reshape(half_heads, slots, LANES)
            if counts is not None:
                scores = scores + bias[None]
            top = jnp.max(scores, axis=1, keepdims=True)
            raised = jnp.exp2((scores - top) * factor)
            total = jnp.sum(raised, axis=1, keepdims=True)
            weights = raised.astype(jnp.bfloat16).reshape(half_heads * slots, LANES)
            v = vals[f : f + LANES, at : at + LANES]
            rolled = pltpu.roll(v, slots, 1)
            v_blocks = []
            for w in range(2):
                twice = (jnp.where(first, v, rolled) if w == 0 else jnp.where(first, rolled, v))
                twice = twice.astype(jnp.bfloat16)
                v_blocks.append(jnp.concatenate([twice * m for m in val_masks], axis=1))
            out = dot(jnp.concatenate(v_blocks, axis=0), weights)
            out = jnp.where(first, out[:LANES], out[LANES:])
            out = out.reshape(half_heads, head_dim, LANES) / total
            halves.append(out.reshape(LANES, LANES).astype(jnp.bfloat16))
        mixed.append(jnp.concatenate(halves, axis=0))
    mixed = jnp.concatenate(mixed, axis=1)
    projected = dot(w_out, mixed)
    hidden = layer_norm(x.astype(jnp.float32).T + projected, 0).astype(jnp.bfloat16)
    lifted = jax.nn.relu(dot(w_up, hidden)).astype(jnp.bfloat16)
    lowered = dot(w_down, lifted)
    return layer_norm(hidden.astype(jnp.float32) + lowered, 0)


def voxel_kernel(
    count_ref, x_ref, cell_ref, qv_ref, k_ref, out_ref, up_ref, down_ref, pooled_ref, acc, enc
):
    step = pl.program_id(0)
    per_step = x_ref.shape[0] * 2 // LANES

    @pl.when(step == 0)
    def _():
        acc[...] = jnp.zeros_like(acc)

    enc[...] = attend_columns(
        x_ref[...],
        lambda w: count_ref[step * per_step + w],
        qv_ref[...],
        k_ref[...],
        out_ref[...],
        up_ref[...],
        down_ref[...],
    ).astype(jnp.bfloat16)
    block = 2 * LANES
    row = lax.broadcasted_iota(jnp.int32, (block, x_ref.shape[0]), 0)

    def pool(i, carry):
        at = pl.multiple_of(i * block, block)
        hot = jnp.where(row == cell_ref[0] - at, 1.0, 0.0).astype(jnp.bfloat16)
        acc[pl.ds(at, block), :] += dot(hot, enc[...], (1, 1))
        return carry

    lax.fori_loop(0, acc.shape[0] // block, pool, 0)

    @pl.when(step == pl.num_programs(0) - 1)
    def _():
        pooled_ref[...] = acc[...].astype(jnp.bfloat16)


def whole(array):
    return pl.BlockSpec(array.shape, lambda *_: (0,) * array.ndim)


def turned_weights(w_qkv, w_out, w_up, w_down):
    width = w_out.shape[0]
    w_qv = jnp.concatenate([w_qkv[:, :width], w_qkv[:, 2 * width :]], axis=1).T
    return w_qv, w_qkv[:, width : 2 * width], w_out.T, w_up.T, w_down.T


def voxel_pool(feat, counts, target, cells, weights):
    tokens, width = feat.shape
    size = min(512, tokens)
    steps = tokens // size
    return pl.pallas_call(
        voxel_kernel,
        grid_spec=pltpu.PrefetchScalarGridSpec(
            num_scalar_prefetch=1,
            grid=(steps,),
            in_specs=[
                pl.BlockSpec((size, width), lambda i, c: (i, 0)),
                pl.BlockSpec((1, 1, size), lambda i, c: (i, 0, 0)),
            ]
            + [whole(w) for w in weights],
            out_specs=pl.BlockSpec((cells, width), lambda i, c: (0, 0)),
            scratch_shapes=[
                pltpu.VMEM((cells, width), jnp.float32),
                pltpu.VMEM((width, size), jnp.bfloat16),
            ],
        ),
        out_shape=jax.ShapeDtypeStruct((cells, width), jnp.bfloat16),
        name="voxel_pool",
    )(counts, feat, target.reshape(steps, 1, size), *weights)


def bev_kernel(x_ref, qv_ref, k_ref, out_ref, up_ref, down_ref, result_ref):
    result_ref[...] = attend_columns(
        x_ref[...], None, qv_ref[...], k_ref[...], out_ref[...], up_ref[...], down_ref[...]
    ).T.astype(jnp.bfloat16)


def bev_block(x, weights):
    tokens, width = x.shape
    size = min(512, tokens)
    return pl.pallas_call(
        bev_kernel,
        grid=(tokens // size,),
        in_specs=[pl.BlockSpec((size, width), lambda i: (i, 0))] + [whole(w) for w in weights],
        out_specs=pl.BlockSpec((size, width), lambda i: (i, 0)),
        out_shape=jax.ShapeDtypeStruct(x.shape, jnp.bfloat16),
        name="bev_block",
    )(x, *weights)


def shards(
    voxel_feat,
    window_count,
    voxel_cell,
    w_qkv_voxel,
    w_out_voxel,
    w_up_voxel,
    w_down_voxel,
    conv_taps,
    w_qkv_bev,
    w_out_bev,
    w_up_bev,
    w_down_bev,
):
    n_tile = lax.axis_size("tile")
    n_band = lax.axis_size("band")
    rows = WSIDE * n_tile * n_band
    cols = CB * n_tile
    width = voxel_feat.shape[2]
    slot_ids = jnp.arange(voxel_feat.shape[1], dtype=jnp.int32)
    keep = slot_ids[None, :] < window_count[:, None]
    target = jnp.where(keep, voxel_cell, -1)
    partial_value = voxel_pool(
        voxel_feat.reshape(-1, width),
        window_count,
        target,
        rows * CB,
        turned_weights(w_qkv_voxel, w_out_voxel, w_up_voxel, w_down_voxel),
    )
    split_rows = partial_value.reshape(n_tile, n_band, WSIDE, CB, width)
    band = lax.axis_index("band")
    mine = lax.dynamic_index_in_dim(split_rows, band, 1, keepdims=False)
    others = lax.dynamic_index_in_dim(split_rows, 1 - band, 1, keepdims=False)
    received = swapped(others, "band", 0)
    strip_part = layer_norm(mine.astype(jnp.float32) + received.astype(jnp.float32)).astype(
        jnp.bfloat16
    )
    arrived = lax.all_to_all(strip_part, "tile", split_axis=0, concat_axis=2, tiled=True)
    bev = arrived.reshape(WSIDE, cols, width)
    extended = with_halo(bev, ((("tile", "band"), 0),), 1)
    padded = jnp.pad(extended, ((0, 0), (1, 1), (0, 0)))
    position = jnp.zeros((WSIDE, cols, width), jnp.float32)
    for row_tap in range(3):
        for col_tap in range(3):
            position = (
                position
                + padded[row_tap : row_tap + WSIDE, col_tap : col_tap + cols].astype(jnp.float32)
                * conv_taps[3 * row_tap + col_tap]
            )
    shaped = (bev.astype(jnp.float32) + position).astype(jnp.bfloat16)
    across = cols // WSIDE
    windows = (
        shaped.reshape(WSIDE, across, WSIDE, width)
        .transpose(1, 0, 2, 3)
        .reshape(across * WSIDE * WSIDE, width)
    )
    result = bev_block(windows, turned_weights(w_qkv_bev, w_out_bev, w_up_bev, w_down_bev))
    return (
        result.reshape(across, WSIDE, WSIDE, width)
        .transpose(1, 0, 2, 3)
        .reshape(WSIDE, cols, width)
    )


def solution(mesh):
    placed = (
        P(("tile", "band"), None, None),
        P(("tile", "band")),
        P(("tile", "band"), None),
        P(),
        P(),
        P(),
        P(),
        P(),
        P(),
        P(),
        P(),
        P(),
    )
    return jax.shard_map(
        shards,
        mesh=mesh,
        in_specs=placed,
        out_specs=P(("tile", "band"), None, None),
        check_vma=False,
    )
```

```python
import functools
import math

import jax
import jax.numpy as jnp
from jax import lax
from jax.experimental import pallas as pl
from jax.experimental.pallas import tpu as pltpu
from jax.sharding import PartitionSpec as P

HEADS = 8
WSIDE = 8
CB = 8
LANES = 128


def layer_norm(values, axis=-1):
    center = values - jnp.mean(values, axis=axis, keepdims=True)
    spread = jnp.mean(center * center, axis=axis, keepdims=True)
    return center * lax.rsqrt(spread + 1e-05)


def dot(a, b, contract=(1, 0)):
    return lax.dot_general(
        a, b, (((contract[0],), (contract[1],)), ((), ())), preferred_element_type=jnp.float32
    )


def attend_columns(x, counts, w_qv, w_k, w_out, w_up, w_down):
    tokens, width = x.shape
    head_dim = width // HEADS
    half_heads = LANES // head_dim
    slots = LANES // 2
    factor = head_dim ** (-0.5) * math.log2(math.e)
    turned = dot(w_qv, x, (1, 1))
    queries = turned[:width].astype(jnp.bfloat16)
    vals = turned[width:]
    keys = dot(x, w_k).astype(jnp.bfloat16)
    lane = lax.broadcasted_iota(jnp.int32, (LANES, LANES), 1)
    row = lax.broadcasted_iota(jnp.int32, (LANES, LANES), 0)
    first = lane < slots
    first_b = first.astype(jnp.bfloat16)
    second_b = 1 - first_b
    key_head = lane[:slots] // head_dim
    key_masks = [(key_head == h).astype(jnp.bfloat16) for h in range(half_heads)]
    val_masks = [
        (row // head_dim == 2 * j + lane // slots).astype(jnp.bfloat16)
        for j in range(half_heads // 2)
    ]
    mixed = []
    for pair in range(tokens // LANES):
        at = pair * LANES
        if counts is not None:
            limit = jnp.where(first[:slots], counts(2 * pair), counts(2 * pair + 1))
            bias = jnp.where(row[:slots] < limit, 0.0, -1e30)
        halves = []
        for half in range(width // LANES):
            f = half * LANES
            q = queries[f : f + LANES, at : at + LANES]
            q_blocks = jnp.concatenate([q * first_b, q * second_b], axis=0)
            k_blocks = jnp.concatenate(
                [
                    jnp.concatenate(
                        [
                            keys[at + w * slots : at + (w + 1) * slots, f : f + LANES] * m
                            for m in key_masks
                        ],
                        axis=0,
                    )
                    for w in range(2)
                ],
                axis=1,
            )
            scores = dot(k_blocks, q_blocks).reshape(half_heads, slots, LANES)
            if counts is not None:
                scores = scores + bias[None]
            top = jnp.max(scores, axis=1, keepdims=True)
            raised = jnp.exp2((scores - top) * factor)
            total = jnp.sum(raised, axis=1, keepdims=True)
            weights = raised.astype(jnp.bfloat16).reshape(half_heads * slots, LANES)
            v = vals[f : f + LANES, at : at + LANES]
            rolled = pltpu.roll(v, slots, 1)
            v_blocks = []
            for w in range(2):
                twice = (jnp.where(first, v, rolled) if w == 0 else jnp.where(first, rolled, v))
                twice = twice.astype(jnp.bfloat16)
                v_blocks.append(jnp.concatenate([twice * m for m in val_masks], axis=1))
            out = dot(jnp.concatenate(v_blocks, axis=0), weights)
            out = jnp.where(first, out[:LANES], out[LANES:])
            out = out.reshape(half_heads, head_dim, LANES) / total
            halves.append(out.reshape(LANES, LANES).astype(jnp.bfloat16))
        mixed.append(jnp.concatenate(halves, axis=0))
    mixed = jnp.concatenate(mixed, axis=1)
    projected = dot(w_out, mixed)
    hidden = layer_norm(x.astype(jnp.float32).T + projected, 0).astype(jnp.bfloat16)
    lifted = jax.nn.relu(dot(w_up, hidden)).astype(jnp.bfloat16)
    lowered = dot(w_down, lifted)
    return layer_norm(hidden.astype(jnp.float32) + lowered, 0)


def turn_weights(qkv_ref, out_ref, up_ref, down_ref, qv_s, out_s, up_s, down_s):
    width = out_ref.shape[0]

    def turned(values):
        return values.astype(jnp.float32).T.astype(jnp.bfloat16)

    qv_s[:width, :] = turned(qkv_ref[:, :width])
    qv_s[width:, :] = turned(qkv_ref[:, 2 * width :])
    out_s[...] = turned(out_ref[...])
    up_s[...] = turned(up_ref[...])
    down_s[...] = turned(down_ref[...])


def turned_scratch(w_qkv, w_out, w_up, w_down):
    width = w_out.shape[0]
    return [
        pltpu.VMEM((2 * width, width), jnp.bfloat16),
        pltpu.VMEM(w_out.shape[::-1], jnp.bfloat16),
        pltpu.VMEM(w_up.shape[::-1], jnp.bfloat16),
        pltpu.VMEM(w_down.shape[::-1], jnp.bfloat16),
    ]


def whole(array):
    return pl.BlockSpec(array.shape, lambda *_: (0,) * array.ndim)


def voxel_kernel(
    count_ref, x_ref, qkv_ref, out_ref, up_ref, down_ref, enc_ref, qv_s, out_s, up_s, down_s
):
    step = pl.program_id(0)
    per_step = x_ref.shape[0] * 2 // LANES
    width = x_ref.shape[1]

    @pl.when(step == 0)
    def _():
        turn_weights(qkv_ref, out_ref, up_ref, down_ref, qv_s, out_s, up_s, down_s)

    enc_ref[0] = attend_columns(
        x_ref[...],
        lambda w: count_ref[step * per_step + w],
        qv_s[...],
        qkv_ref[:, width : 2 * width],
        out_s[...],
        up_s[...],
        down_s[...],
    ).astype(jnp.bfloat16)


def voxel_block(feat, counts, weights):
    tokens, width = feat.shape
    size = min(512, tokens)
    steps = tokens // size
    return pl.pallas_call(
        voxel_kernel,
        grid_spec=pltpu.PrefetchScalarGridSpec(
            num_scalar_prefetch=1,
            grid=(steps,),
            in_specs=[pl.BlockSpec((size, width), lambda i, c: (i, 0))]
            + [whole(w) for w in weights],
            out_specs=pl.BlockSpec((1, width, size), lambda i, c: (i, 0, 0)),
            scratch_shapes=turned_scratch(*weights),
        ),
        out_shape=jax.ShapeDtypeStruct((steps, width, size), jnp.bfloat16),
        name="voxel_block",
    )(counts, feat, *weights)


def pool_kernel(
    n_tile,
    n_band,
    cell_ref,
    enc_ref,
    grid_ref,
    low_ref,
    high_ref,
    acc,
    mine,
    theirs,
    came,
    ready,
    landed,
    low,
    high,
    swap_send,
    swap_recv,
    send,
    recv,
    halo_send,
    halo_recv,
):
    tile = lax.axis_index("tile")
    band = lax.axis_index("band")
    other = 1 - band
    strip = tile * n_band + band
    chunks, width, size = enc_ref.shape
    blocks = mine.shape[0]
    per = n_tile // blocks
    cells = WSIDE * CB
    block = acc.shape[0]
    mesh_id = pl.DeviceIdType.MESH

    def strip_id(s):
        return (s // n_band, s % n_band)

    barrier = pltpu.get_barrier_semaphore()

    def greet(i, carry):
        peer = lax.rem(tile + i, n_tile)
        pl.semaphore_signal(barrier, inc=1, device_id=(peer, band), device_id_type=mesh_id)
        return carry

    lax.fori_loop(1, n_tile, greet, 0)
    pl.semaphore_signal(barrier, inc=1, device_id=(tile, other), device_id_type=mesh_id)
    across_below = jnp.logical_and(band == 0, tile > 0)
    across_above = jnp.logical_and(band == n_band - 1, tile < n_tile - 1)

    @pl.when(across_below)
    def _():
        pl.semaphore_signal(barrier, inc=1, device_id=strip_id(strip - 1), device_id_type=mesh_id)

    @pl.when(across_above)
    def _():
        pl.semaphore_signal(barrier, inc=1, device_id=strip_id(strip + 1), device_id_type=mesh_id)

    across = jnp.logical_or(across_below, across_above)

    @pl.when(across)
    def _():
        pl.semaphore_wait(barrier, n_tile + 1)

    @pl.when(jnp.logical_not(across))
    def _():
        pl.semaphore_wait(barrier, n_tile)

    row = lax.broadcasted_iota(jnp.int32, (block, size), 0)

    def place(i):
        return lax.rem(tile // per + 1 + i, blocks)

    def swap(j):
        return pltpu.make_async_remote_copy(
            src_ref=theirs.at[j],
            dst_ref=came.at[j],
            send_sem=swap_send.at[j],
            recv_sem=swap_recv.at[j],
            device_id=(tile, other),
            device_id_type=mesh_id,
        )

    def deliver(dest, source):
        return pltpu.make_async_remote_copy(
            src_ref=ready.at[dest],
            dst_ref=landed.at[source],
            send_sem=send.at[dest],
            recv_sem=recv.at[source],
            device_id=(dest, band),
            device_id_type=mesh_id,
        )

    def compute(i):
        j = place(i)
        acc[...] = jnp.zeros_like(acc)
        together = 2 if chunks % 2 == 0 else 1

        def add(c, carry):
            term = None
            for k in range(together):
                hot = jnp.where(row == cell_ref[together * c + k] - j * block, 1.0, 0.0)
                part = dot(hot.astype(jnp.bfloat16), enc_ref[together * c + k], (1, 1))
                term = part if term is None else term + part
            acc[...] += term
            return carry

        lax.fori_loop(0, chunks // together, add, 0)
        for d in range(per):
            at = d * n_band * cells
            mine[j, d * cells : (d + 1) * cells, :] = acc[
                pl.ds(pl.multiple_of(at + band * cells, cells), cells), :
            ].astype(jnp.bfloat16)
            theirs[j, d * cells : (d + 1) * cells, :] = acc[
                pl.ds(pl.multiple_of(at + other * cells, cells), cells), :
            ].astype(jnp.bfloat16)
        swap(j).start()

    def finish(i):
        j = place(i)
        swap(j).wait_recv()
        total = mine[j].astype(jnp.float32) + came[j].astype(jnp.float32)
        normal = layer_norm(total).reshape(per, WSIDE, CB, width).astype(jnp.bfloat16)
        for d in range(per):
            dest = j * per + d

            @pl.when(dest != tile)
            def _():
                ready[dest] = normal[d]
                deliver(dest, tile).start()

            @pl.when(dest == tile)
            def _():
                landed[tile] = normal[d]

    compute(0)

    def both(i, carry):
        compute(i)
        finish(i - 1)
        return carry

    lax.fori_loop(1, blocks, both, 0)
    finish(blocks - 1)

    def arrive(i, carry):
        peer = lax.rem(tile + i, n_tile)
        deliver(peer, peer).wait_recv()
        return carry

    lax.fori_loop(1, n_tile, arrive, 0)

    def edge(side, target):
        return pltpu.make_async_remote_copy(
            src_ref=landed.at[:, 0 if side == 0 else WSIDE - 1],
            dst_ref=high if side == 0 else low,
            send_sem=halo_send.at[side],
            recv_sem=halo_recv.at[side],
            device_id=strip_id(target),
            device_id_type=mesh_id,
        )

    has_below = strip > 0
    has_above = strip < n_tile * n_band - 1

    @pl.when(has_below)
    def _():
        edge(0, strip - 1).start()

    @pl.when(has_above)
    def _():
        edge(1, strip + 1).start()

    grid_ref[...] = landed[...]

    def left(i, carry):
        peer = lax.rem(tile + i, n_tile)
        deliver(peer, peer).wait_send()
        return carry

    lax.fori_loop(1, n_tile, left, 0)

    def swapped(j, carry):
        swap(j).wait_send()
        return carry

    lax.fori_loop(0, blocks, swapped, 0)

    @pl.when(has_below)
    def _():
        edge(0, strip - 1).wait_send()
        edge(1, strip - 1).wait_recv()
        low_ref[...] = low[...]

    @pl.when(has_above)
    def _():
        edge(1, strip + 1).wait_send()
        edge(0, strip + 1).wait_recv()
        high_ref[...] = high[...]

    @pl.when(strip == 0)
    def _():
        low_ref[...] = jnp.zeros_like(low_ref)

    @pl.when(strip == n_tile * n_band - 1)
    def _():
        high_ref[...] = jnp.zeros_like(high_ref)


def pool_exchange(encoded, target, n_tile, n_band):
    chunks, width, size = encoded.shape
    cells = WSIDE * CB
    per = 2 if n_tile % 2 == 0 else 1
    blocks = n_tile // per
    half = jnp.bfloat16
    vmem = pl.BlockSpec(memory_space=pltpu.VMEM)
    return pl.pallas_call(
        functools.partial(pool_kernel, n_tile, n_band),
        in_specs=[vmem] * 2,
        out_specs=[vmem] * 3,
        out_shape=[
            jax.ShapeDtypeStruct((n_tile, WSIDE, CB, width), half),
            jax.ShapeDtypeStruct((n_tile, CB, width), half),
            jax.ShapeDtypeStruct((n_tile, CB, width), half),
        ],
        scratch_shapes=[
            pltpu.VMEM((per * n_band * cells, width), jnp.float32),
            pltpu.VMEM((blocks, per * cells, width), half),
            pltpu.VMEM((blocks, per * cells, width), half),
            pltpu.VMEM((blocks, per * cells, width), half),
            pltpu.VMEM((n_tile, WSIDE, CB, width), half),
            pltpu.VMEM((n_tile, WSIDE, CB, width), half),
            pltpu.VMEM((n_tile, CB, width), half),
            pltpu.VMEM((n_tile, CB, width), half),
            pltpu.SemaphoreType.DMA((blocks,)),
            pltpu.SemaphoreType.DMA((blocks,)),
            pltpu.SemaphoreType.DMA((n_tile,)),
            pltpu.SemaphoreType.DMA((n_tile,)),
            pltpu.SemaphoreType.DMA((2,)),
            pltpu.SemaphoreType.DMA((2,)),
        ],
        compiler_params=pltpu.CompilerParams(collective_id=0, has_side_effects=True),
        name="pool_exchange",
    )(target.reshape(chunks, 1, size), encoded)


def bev_kernel(
    grid_ref,
    low_ref,
    high_ref,
    tap_ref,
    qkv_ref,
    out_ref,
    up_ref,
    down_ref,
    result_ref,
    wide,
    qv_s,
    out_s,
    up_s,
    down_s,
):
    step = pl.program_id(0)
    n_tile, _, _, width = grid_ref.shape
    span = result_ref.shape[1]

    @pl.when(step == 0)
    def _():
        turn_weights(qkv_ref, out_ref, up_ref, down_ref, qv_s, out_s, up_s, down_s)
        edge = jnp.zeros((WSIDE + 2, CB, width), jnp.float32)
        wide[:, :CB, :] = edge
        wide[:, (n_tile + 1) * CB :, :] = edge

        def fill(t, carry):
            to = pl.ds(pl.multiple_of((t + 1) * CB, CB), CB)
            wide[0, to, :] = low_ref[t].astype(jnp.float32)
            wide[WSIDE + 1, to, :] = high_ref[t].astype(jnp.float32)
            wide[1 : WSIDE + 1, to, :] = grid_ref[t].astype(jnp.float32)
            return carry

        lax.fori_loop(0, n_tile, fill, 0)

    at = pl.multiple_of(step * span, span)
    sums = [jnp.zeros((span, width), jnp.float32) for _ in range(WSIDE)]
    centers = []
    for r in range(WSIDE + 2):
        slab = wide[r, pl.ds(at, span + 2 * CB), :]
        for c in range(3):
            moved = slab[CB + c - 1 : CB + c - 1 + span]
            if c == 1:
                centers.append(moved)
            for row_tap in range(3):
                to = r - row_tap
                if 0 <= to < WSIDE:
                    tap = tap_ref[3 * row_tap + c : 3 * row_tap + c + 1, :]
                    sums[to] = sums[to] + moved * tap
    shaped = [centers[r + 1] + sums[r] for r in range(WSIDE)]
    count = span // CB
    x = jnp.concatenate(
        [shaped[r][w * CB : (w + 1) * CB] for w in range(count) for r in range(WSIDE)], axis=0
    ).astype(jnp.bfloat16)
    result = attend_columns(
        x, None, qv_s[...], qkv_ref[:, width : 2 * width], out_s[...], up_s[...], down_s[...]
    ).T
    for r in range(WSIDE):
        result_ref[r] = jnp.concatenate(
            [result[(w * WSIDE + r) * CB : (w * WSIDE + r + 1) * CB] for w in range(count)], axis=0
        ).astype(jnp.bfloat16)


def bev_block(grid, low, high, taps, weights):
    n_tile, _, _, width = grid.shape
    cols = n_tile * CB
    span = min(64, cols)
    inputs = (grid, low, high, taps, *weights)
    return pl.pallas_call(
        bev_kernel,
        grid=(cols // span,),
        in_specs=[whole(a) for a in inputs],
        out_specs=pl.BlockSpec((WSIDE, span, width), lambda i: (0, i, 0)),
        out_shape=jax.ShapeDtypeStruct((WSIDE, cols, width), jnp.bfloat16),
        scratch_shapes=[pltpu.VMEM((WSIDE + 2, cols + 2 * CB, width), jnp.float32)]
        + turned_scratch(*weights),
        name="bev_block",
    )(*inputs)


def shards(
    voxel_feat,
    window_count,
    voxel_cell,
    w_qkv_voxel,
    w_out_voxel,
    w_up_voxel,
    w_down_voxel,
    conv_taps,
    w_qkv_bev,
    w_out_bev,
    w_up_bev,
    w_down_bev,
):
    n_tile = lax.axis_size("tile")
    n_band = lax.axis_size("band")
    width = voxel_feat.shape[2]
    slot_ids = jnp.arange(voxel_feat.shape[1], dtype=jnp.int32)
    keep = slot_ids[None, :] < window_count[:, None]
    target = jnp.where(keep, voxel_cell, -1)
    encoded = voxel_block(
        voxel_feat.reshape(-1, width),
        window_count,
        (w_qkv_voxel, w_out_voxel, w_up_voxel, w_down_voxel),
    )
    grid, low, high = pool_exchange(encoded, target, n_tile, n_band)
    return bev_block(
        grid, low, high, conv_taps, (w_qkv_bev, w_out_bev, w_up_bev, w_down_bev)
    )


def solution(mesh):
    placed = (
        P(("tile", "band"), None, None),
        P(("tile", "band")),
        P(("tile", "band"), None),
        P(),
        P(),
        P(),
        P(),
        P(),
        P(),
        P(),
        P(),
        P(),
    )
    return jax.shard_map(
        shards,
        mesh=mesh,
        in_specs=placed,
        out_specs=P(("tile", "band"), None, None),
        check_vma=False,
    )
```

```python
import functools
import math

import jax
import jax.numpy as jnp
from jax import lax
from jax.experimental import pallas as pl
from jax.experimental.pallas import tpu as pltpu
from jax.sharding import PartitionSpec as P

HEADS = 8
WSIDE = 8
CB = 8
LANES = 128


def layer_norm(values, axis=-1):
    center = values - jnp.mean(values, axis=axis, keepdims=True)
    spread = jnp.mean(center * center, axis=axis, keepdims=True)
    return center * lax.rsqrt(spread + 1e-05)


def dot(a, b, contract=(1, 0)):
    return lax.dot_general(
        a, b, (((contract[0],), (contract[1],)), ((), ())), preferred_element_type=jnp.float32
    )


def attend_columns(x, counts, w_qv, w_k, w_out, w_up, w_down):
    tokens, width = x.shape
    head_dim = width // HEADS
    half_heads = LANES // head_dim
    slots = LANES // 2
    factor = head_dim ** (-0.5) * math.log2(math.e)
    turned = dot(w_qv, x, (1, 1))
    queries = turned[:width].astype(jnp.bfloat16)
    vals = turned[width:]
    keys = dot(x, w_k).astype(jnp.bfloat16)
    lane = lax.broadcasted_iota(jnp.int32, (LANES, LANES), 1)
    row = lax.broadcasted_iota(jnp.int32, (LANES, LANES), 0)
    first = lane < slots
    first_b = first.astype(jnp.bfloat16)
    second_b = 1 - first_b
    key_head = lane[:slots] // head_dim
    key_masks = [(key_head == h).astype(jnp.bfloat16) for h in range(half_heads)]
    val_masks = [(row // head_dim == h).astype(jnp.bfloat16) for h in range(half_heads)]
    mixed = []
    for pair in range(tokens // LANES):
        at = pair * LANES
        if counts is not None:
            limit = jnp.where(first[:slots], counts(2 * pair), counts(2 * pair + 1))
            bias = jnp.where(row[:slots] < limit, 0.0, -1e30)
        halves = []
        for half in range(width // LANES):
            f = half * LANES
            q = queries[f : f + LANES, at : at + LANES]
            q_blocks = jnp.concatenate([q * first_b, q * second_b], axis=0)
            k_blocks = jnp.concatenate(
                [
                    jnp.concatenate(
                        [
                            keys[at + w * slots : at + (w + 1) * slots, f : f + LANES] * m
                            for m in key_masks
                        ],
                        axis=0,
                    )
                    for w in range(2)
                ],
                axis=1,
            )
            scores = dot(k_blocks, q_blocks).reshape(half_heads, slots, LANES)
            if counts is not None:
                scores = scores + bias[None]
            top = jnp.max(scores, axis=1, keepdims=True)
            raised = jnp.exp2((scores - top) * factor)
            total = jnp.sum(raised, axis=1, keepdims=True)
            weights = raised.astype(jnp.bfloat16).reshape(half_heads * slots, LANES)
            v = vals[f : f + LANES, at : at + LANES].astype(jnp.bfloat16)
            v_blocks = jnp.concatenate([v * m for m in val_masks], axis=1)
            spread = jnp.concatenate(
                [
                    weights[h * slots : (h + 1) * slots] * m
                    for h in range(half_heads)
                    for m in (first_b[:slots], second_b[:slots])
                ],
                axis=0,
            )
            out = dot(v_blocks, spread)
            out = out.reshape(half_heads, head_dim, LANES) / total
            halves.append(out.reshape(LANES, LANES).astype(jnp.bfloat16))
        mixed.append(jnp.concatenate(halves, axis=0))
    mixed = jnp.concatenate(mixed, axis=1)
    projected = dot(w_out, mixed)
    hidden = layer_norm(x.astype(jnp.float32).T + projected, 0).astype(jnp.bfloat16)
    lifted = jax.nn.relu(dot(w_up, hidden)).astype(jnp.bfloat16)
    lowered = dot(w_down, lifted)
    return layer_norm(hidden.astype(jnp.float32) + lowered, 0)


def turn_weights(qkv_ref, out_ref, up_ref, down_ref, qv_s, out_s, up_s, down_s):
    width = out_ref.shape[0]

    def turned(values):
        return values.astype(jnp.float32).T.astype(jnp.bfloat16)

    qv_s[:width, :] = turned(qkv_ref[:, :width])
    qv_s[width:, :] = turned(qkv_ref[:, 2 * width :])
    out_s[...] = turned(out_ref[...])
    up_s[...] = turned(up_ref[...])
    down_s[...] = turned(down_ref[...])


def turned_scratch(w_qkv, w_out, w_up, w_down):
    width = w_out.shape[0]
    return [
        pltpu.VMEM((2 * width, width), jnp.bfloat16),
        pltpu.VMEM(w_out.shape[::-1], jnp.bfloat16),
        pltpu.VMEM(w_up.shape[::-1], jnp.bfloat16),
        pltpu.VMEM(w_down.shape[::-1], jnp.bfloat16),
    ]


def whole(array):
    return pl.BlockSpec(array.shape, lambda *_: (0,) * array.ndim)


def voxel_kernel(
    count_ref, x_ref, qkv_ref, out_ref, up_ref, down_ref, enc_ref, qv_s, out_s, up_s, down_s
):
    step = pl.program_id(0)
    per_step = x_ref.shape[0] * 2 // LANES
    width = x_ref.shape[1]

    @pl.when(step == 0)
    def _():
        turn_weights(qkv_ref, out_ref, up_ref, down_ref, qv_s, out_s, up_s, down_s)

    enc_ref[...] = attend_columns(
        x_ref[...],
        lambda w: count_ref[step * per_step + w],
        qv_s[...],
        qkv_ref[:, width : 2 * width],
        out_s[...],
        up_s[...],
        down_s[...],
    ).T.astype(jnp.bfloat16)


def voxel_block(feat, counts, weights):
    tokens, width = feat.shape
    size = min(512, tokens)
    steps = tokens // size
    return pl.pallas_call(
        voxel_kernel,
        grid_spec=pltpu.PrefetchScalarGridSpec(
            num_scalar_prefetch=1,
            grid=(steps,),
            in_specs=[pl.BlockSpec((size, width), lambda i, c: (i, 0))]
            + [whole(w) for w in weights],
            out_specs=pl.BlockSpec((size, width), lambda i, c: (i, 0)),
            scratch_shapes=turned_scratch(*weights),
        ),
        out_shape=jax.ShapeDtypeStruct((tokens, width), jnp.bfloat16),
        name="voxel_block",
    )(counts, feat, *weights)


def pool_kernel(
    n_tile,
    n_band,
    cell_ref,
    enc_ref,
    grid_ref,
    low_ref,
    high_ref,
    acc,
    mine,
    theirs,
    came,
    ready,
    landed,
    low,
    high,
    swap_send,
    swap_recv,
    send,
    recv,
    halo_send,
    halo_recv,
):
    tile = lax.axis_index("tile")
    band = lax.axis_index("band")
    other = 1 - band
    strip = tile * n_band + band
    chunks, _, size = cell_ref.shape
    width = enc_ref.shape[1]
    blocks = mine.shape[0]
    per = n_tile // blocks
    cells = WSIDE * CB
    block = acc.shape[0]
    mesh_id = pl.DeviceIdType.MESH

    def strip_id(s):
        return (s // n_band, s % n_band)

    barrier = pltpu.get_barrier_semaphore()

    def greet(i, carry):
        peer = lax.rem(tile + i, n_tile)
        pl.semaphore_signal(barrier, inc=1, device_id=(peer, band), device_id_type=mesh_id)
        return carry

    lax.fori_loop(1, n_tile, greet, 0)
    pl.semaphore_signal(barrier, inc=1, device_id=(tile, other), device_id_type=mesh_id)
    across_below = jnp.logical_and(band == 0, tile > 0)
    across_above = jnp.logical_and(band == n_band - 1, tile < n_tile - 1)

    @pl.when(across_below)
    def _():
        pl.semaphore_signal(barrier, inc=1, device_id=strip_id(strip - 1), device_id_type=mesh_id)

    @pl.when(across_above)
    def _():
        pl.semaphore_signal(barrier, inc=1, device_id=strip_id(strip + 1), device_id_type=mesh_id)

    across = jnp.logical_or(across_below, across_above)

    @pl.when(across)
    def _():
        pl.semaphore_wait(barrier, n_tile + 1)

    @pl.when(jnp.logical_not(across))
    def _():
        pl.semaphore_wait(barrier, n_tile)

    row = lax.broadcasted_iota(jnp.int32, (block, size), 0)

    def place(i):
        ahead = jnp.where(i < blocks - blocks // 2, blocks // 2 + i, blocks - 1 - i)
        return lax.rem(tile // per + ahead, blocks)

    def swap(j):
        return pltpu.make_async_remote_copy(
            src_ref=theirs.at[j],
            dst_ref=came.at[j],
            send_sem=swap_send.at[j],
            recv_sem=swap_recv.at[j],
            device_id=(tile, other),
            device_id_type=mesh_id,
        )

    def deliver(dest, source):
        return pltpu.make_async_remote_copy(
            src_ref=ready.at[dest],
            dst_ref=landed.at[source],
            send_sem=send.at[dest],
            recv_sem=recv.at[source],
            device_id=(dest, band),
            device_id_type=mesh_id,
        )

    def compute(i):
        j = place(i)
        acc[...] = jnp.zeros_like(acc)
        together = math.gcd(chunks, 8)

        def add(c, carry):
            term = None
            for k in range(together):
                hot = jnp.where(row == cell_ref[together * c + k] - j * block, 1.0, 0.0)
                at = pl.multiple_of((together * c + k) * size, size)
                part = dot(hot.astype(jnp.bfloat16), enc_ref[pl.ds(at, size), :])
                term = part if term is None else term + part
            acc[...] += term
            return carry

        lax.fori_loop(0, chunks // together, add, 0)
        for d in range(per):
            at = d * n_band * cells
            mine[j, d * cells : (d + 1) * cells, :] = acc[
                pl.ds(pl.multiple_of(at + band * cells, cells), cells), :
            ].astype(jnp.bfloat16)
            theirs[j, d * cells : (d + 1) * cells, :] = acc[
                pl.ds(pl.multiple_of(at + other * cells, cells), cells), :
            ].astype(jnp.bfloat16)
        swap(j).start()

    def finish(i):
        j = place(i)
        swap(j).wait_recv()
        total = mine[j].astype(jnp.float32) + came[j].astype(jnp.float32)
        normal = layer_norm(total).reshape(per, WSIDE, CB, width).astype(jnp.bfloat16)
        for d in range(per):
            dest = j * per + d

            @pl.when(dest != tile)
            def _():
                ready[dest] = normal[d]
                deliver(dest, tile).start()

            @pl.when(dest == tile)
            def _():
                landed[tile] = normal[d]

    compute(0)

    def both(i, carry):
        compute(i)
        finish(i - 1)
        return carry

    lax.fori_loop(1, blocks, both, 0)
    finish(blocks - 1)

    def arrive(i, carry):
        peer = lax.rem(tile + i, n_tile)
        deliver(peer, peer).wait_recv()
        return carry

    lax.fori_loop(1, n_tile, arrive, 0)

    def edge(side, target):
        return pltpu.make_async_remote_copy(
            src_ref=landed.at[:, 0 if side == 0 else WSIDE - 1],
            dst_ref=high if side == 0 else low,
            send_sem=halo_send.at[side],
            recv_sem=halo_recv.at[side],
            device_id=strip_id(target),
            device_id_type=mesh_id,
        )

    has_below = strip > 0
    has_above = strip < n_tile * n_band - 1

    @pl.when(has_below)
    def _():
        edge(0, strip - 1).start()

    @pl.when(has_above)
    def _():
        edge(1, strip + 1).start()

    grid_ref[...] = landed[...]

    def left(i, carry):
        peer = lax.rem(tile + i, n_tile)
        deliver(peer, peer).wait_send()
        return carry

    lax.fori_loop(1, n_tile, left, 0)

    def swapped(j, carry):
        swap(j).wait_send()
        return carry

    lax.fori_loop(0, blocks, swapped, 0)

    @pl.when(has_below)
    def _():
        edge(0, strip - 1).wait_send()
        edge(1, strip - 1).wait_recv()
        low_ref[...] = low[...]

    @pl.when(has_above)
    def _():
        edge(1, strip + 1).wait_send()
        edge(0, strip + 1).wait_recv()
        high_ref[...] = high[...]

    @pl.when(strip == 0)
    def _():
        low_ref[...] = jnp.zeros_like(low_ref)

    @pl.when(strip == n_tile * n_band - 1)
    def _():
        high_ref[...] = jnp.zeros_like(high_ref)


def pool_exchange(encoded, target, n_tile, n_band):
    tokens, width = encoded.shape
    size = min(512, tokens)
    chunks = tokens // size
    cells = WSIDE * CB
    per = math.gcd(n_tile, 4)
    blocks = n_tile // per
    half = jnp.bfloat16
    vmem = pl.BlockSpec(memory_space=pltpu.VMEM)
    return pl.pallas_call(
        functools.partial(pool_kernel, n_tile, n_band),
        in_specs=[vmem] * 2,
        out_specs=[vmem] * 3,
        out_shape=[
            jax.ShapeDtypeStruct((n_tile, WSIDE, CB, width), half),
            jax.ShapeDtypeStruct((n_tile, CB, width), half),
            jax.ShapeDtypeStruct((n_tile, CB, width), half),
        ],
        scratch_shapes=[
            pltpu.VMEM((per * n_band * cells, width), jnp.float32),
            pltpu.VMEM((blocks, per * cells, width), half),
            pltpu.VMEM((blocks, per * cells, width), half),
            pltpu.VMEM((blocks, per * cells, width), half),
            pltpu.VMEM((n_tile, WSIDE, CB, width), half),
            pltpu.VMEM((n_tile, WSIDE, CB, width), half),
            pltpu.VMEM((n_tile, CB, width), half),
            pltpu.VMEM((n_tile, CB, width), half),
            pltpu.SemaphoreType.DMA((blocks,)),
            pltpu.SemaphoreType.DMA((blocks,)),
            pltpu.SemaphoreType.DMA((n_tile,)),
            pltpu.SemaphoreType.DMA((n_tile,)),
            pltpu.SemaphoreType.DMA((2,)),
            pltpu.SemaphoreType.DMA((2,)),
        ],
        compiler_params=pltpu.CompilerParams(collective_id=0, has_side_effects=True),
        name="pool_exchange",
    )(target.reshape(chunks, 1, size), encoded)


def bev_kernel(
    grid_ref,
    low_ref,
    high_ref,
    tap_ref,
    qkv_ref,
    out_ref,
    up_ref,
    down_ref,
    result_ref,
    wide,
    qv_s,
    out_s,
    up_s,
    down_s,
):
    step = pl.program_id(0)
    n_tile, _, _, width = grid_ref.shape
    span = result_ref.shape[1]

    @pl.when(step == 0)
    def _():
        turn_weights(qkv_ref, out_ref, up_ref, down_ref, qv_s, out_s, up_s, down_s)
        edge = jnp.zeros((WSIDE + 2, CB, width), jnp.float32)
        wide[:, :CB, :] = edge
        wide[:, (n_tile + 1) * CB :, :] = edge

        def fill(t, carry):
            to = pl.ds(pl.multiple_of((t + 1) * CB, CB), CB)
            wide[0, to, :] = low_ref[t].astype(jnp.float32)
            wide[WSIDE + 1, to, :] = high_ref[t].astype(jnp.float32)
            wide[1 : WSIDE + 1, to, :] = grid_ref[t].astype(jnp.float32)
            return carry

        lax.fori_loop(0, n_tile, fill, 0)

    at = pl.multiple_of(step * span, span)
    sums = [jnp.zeros((span, width), jnp.float32) for _ in range(WSIDE)]
    centers = []
    for r in range(WSIDE + 2):
        slab = wide[r, pl.ds(at, span + 2 * CB), :]
        for c in range(3):
            moved = slab[CB + c - 1 : CB + c - 1 + span]
            if c == 1:
                centers.append(moved)
            for row_tap in range(3):
                to = r - row_tap
                if 0 <= to < WSIDE:
                    tap = tap_ref[3 * row_tap + c : 3 * row_tap + c + 1, :]
                    sums[to] = sums[to] + moved * tap
    shaped = [centers[r + 1] + sums[r] for r in range(WSIDE)]
    count = span // CB
    x = jnp.concatenate(
        [shaped[r][w * CB : (w + 1) * CB] for w in range(count) for r in range(WSIDE)], axis=0
    ).astype(jnp.bfloat16)
    result = attend_columns(
        x, None, qv_s[...], qkv_ref[:, width : 2 * width], out_s[...], up_s[...], down_s[...]
    ).T
    for r in range(WSIDE):
        result_ref[r] = jnp.concatenate(
            [result[(w * WSIDE + r) * CB : (w * WSIDE + r + 1) * CB] for w in range(count)], axis=0
        ).astype(jnp.bfloat16)


def bev_block(grid, low, high, taps, weights):
    n_tile, _, _, width = grid.shape
    cols = n_tile * CB
    span = min(64, cols)
    inputs = (grid, low, high, taps, *weights)
    return pl.pallas_call(
        bev_kernel,
        grid=(cols // span,),
        in_specs=[whole(a) for a in inputs],
        out_specs=pl.BlockSpec((WSIDE, span, width), lambda i: (0, i, 0)),
        out_shape=jax.ShapeDtypeStruct((WSIDE, cols, width), jnp.bfloat16),
        scratch_shapes=[pltpu.VMEM((WSIDE + 2, cols + 2 * CB, width), jnp.float32)]
        + turned_scratch(*weights),
        name="bev_block",
    )(*inputs)


def shards(
    voxel_feat,
    window_count,
    voxel_cell,
    w_qkv_voxel,
    w_out_voxel,
    w_up_voxel,
    w_down_voxel,
    conv_taps,
    w_qkv_bev,
    w_out_bev,
    w_up_bev,
    w_down_bev,
):
    n_tile = lax.axis_size("tile")
    n_band = lax.axis_size("band")
    width = voxel_feat.shape[2]
    slot_ids = jnp.arange(voxel_feat.shape[1], dtype=jnp.int32)
    keep = slot_ids[None, :] < window_count[:, None]
    target = jnp.where(keep, voxel_cell, -1)
    encoded = voxel_block(
        voxel_feat.reshape(-1, width),
        window_count,
        (w_qkv_voxel, w_out_voxel, w_up_voxel, w_down_voxel),
    )
    grid, low, high = pool_exchange(encoded, target, n_tile, n_band)
    return bev_block(
        grid, low, high, conv_taps, (w_qkv_bev, w_out_bev, w_up_bev, w_down_bev)
    )


def solution(mesh):
    placed = (
        P(("tile", "band"), None, None),
        P(("tile", "band")),
        P(("tile", "band"), None),
        P(),
        P(),
        P(),
        P(),
        P(),
        P(),
        P(),
        P(),
        P(),
    )
    return jax.shard_map(
        shards,
        mesh=mesh,
        in_specs=placed,
        out_specs=P(("tile", "band"), None, None),
        check_vma=False,
    )
```
